1024 devices in a mesh: dp: 32 (over z_lo, core), tp: 32 (over y, x, z_hi).
Axes of the slice: x: 4, y: 4, z: 32 (z_hi: 2, z_lo: 16; z = z_hi * 16 + z_lo), core: 2. Of those that a mesh axis runs over, the one named last changes fastest.
Arguments:
- out_grad: bfloat16 [4096, 7168], P(('dp', 'tp')), may hold values from -6 to 6
- gate_pre: bfloat16 [4096, 12288], P('dp', 'tp'), may hold values from -8 to 8
- up_pre: bfloat16 [4096, 12288], P('dp', 'tp'), may hold values from -6 to 6
- down_weight: bfloat16 [7168, 12288], P(None, 'tp'), may hold values from -0.0625 to 0.0625
- block_scales: bfloat16 [56, 96], P(None, 'tp'), may hold values from 0.25 to 4
Outputs:
- gate_grad: bfloat16 [4096, 12288], P('dp', 'tp')
- up_grad: bfloat16 [4096, 12288], P('dp', 'tp')
- down_grad: bfloat16 [7168, 12288], P('dp', 'tp')
The draws below stay inside these ranges and needn't reach their ends.
All inputs are finite; a program needn't handle non-finite values.
Results may differ from the reference program's by a relative error of at most 0.028.
Values may be sent and summed in bfloat16 or wider, within the bound.
A program may use at most 64 MiB of HBM per device.

```python
import math
import jax
import jax.numpy as jnp
from jax import lax

D = 7168
FF = 12288
TOK = 128
TOKENS = 4096
N_DP = 32


def strengthened(values, key, source, target, blocks, factor):
    owner, partner = [(jnp.arange(values.shape[position]) // (values.shape[position] // blocks)).reshape([-1 if axis == position else 1 for axis in range(values.ndim)]) for position in (source, target)]
    chosen = jax.random.permutation(key, blocks)[partner]
    strong = (owner == chosen) | (owner == (partner + blocks // 2) % blocks)
    return jnp.where(strong, factor * values, values)


def level_of(stream_key, dims, cuts, smallest, high):
    def one(dim, blocks):
        steps = jax.random.uniform(jax.random.fold_in(jax.random.fold_in(stream_key, 6), dim), (blocks,), jnp.float32, smallest / len(cuts), high / len(cuts))
        return jnp.repeat(jnp.exp(steps), dims[dim] // blocks).reshape((-1,) + (1,) * (len(dims) - dim - 1))

    gain = one(*cuts[0])
    for cut in cuts[1:]:
        gain = gain * one(*cut)
    return gain


def normal_values(rng, dims, deviation, most, split=(), held_as=jnp.bfloat16):
    factor_of = level_of(rng, dims, split, -0.22, 0.18) if split else 1.0
    array = jax.random.normal(rng, dims, jnp.float32) * deviation * factor_of
    return jnp.minimum(jnp.maximum(array, -most), most).astype(held_as)


def gaussian_with(key, dims, scale, most, pieces, heavy, kind=jnp.bfloat16):
    entries = scale * jax.random.normal(key, dims, jnp.float32)
    if pieces:
        entries = entries * level_of(key, dims, pieces, -0.22, 0.18)
    return jnp.clip(strengthened(entries, jax.random.fold_in(key, 3), *heavy), -most, most).astype(kind)


def setup_inputs(seed: int = 0) -> dict:
    seeds = jax.random.split(jax.random.key(seed), 6)
    return {
        "out_grad": gaussian_with(seeds[0], (TOKENS, D), 0.25, 6.0, ((0, 1024),), (0, 1, 1024, 6.0)),
        "gate_pre": normal_values(seeds[1], (TOKENS, FF), 1.5, 8.0, ((0, 32), (1, 32))),
        "up_pre": normal_values(seeds[2], (TOKENS, FF), 1.0, 6.0, ((0, 32), (1, 32))),
        "down_weight": normal_values(seeds[3], (D, FF), D ** -0.5, 0.0625, ((1, 32),)),
        "block_scales": jnp.clip(jnp.exp(math.log(4.0) - 2.7725887 * jax.random.uniform(seeds[4], (D // 128, FF // 128), jnp.float32) ** level_of(seeds[4], (D // 128, FF // 128), ((1, 32),), -0.2, 0.2)), 0.25, 4.0).astype(jnp.bfloat16),
    }


def tile_quant(values, tile_axis):
    largest = jnp.max(jnp.abs(values), axis=tile_axis, keepdims=True)
    tile_scale = (largest + 1e-6) / 448.0
    payload = (values / tile_scale).astype(jnp.bfloat16)
    return (payload.astype(jnp.float32) * tile_scale).astype(jnp.bfloat16)


def reference(out_grad, gate_pre, up_pre, down_weight, block_scales):
    width = down_weight.shape[0]
    hidden_units = down_weight.shape[1]
    total = out_grad.shape[0]
    weight_deq = (down_weight.reshape(width // 128, 128, hidden_units // 128, 128)
                  * block_scales[:, None, :, None]).reshape(width, hidden_units).astype(jnp.bfloat16)
    grad_full = out_grad.astype(jnp.float32)
    grad_rowq = tile_quant(grad_full.reshape(total, width // 128, 128), 2).reshape(total, width)
    grad_colq = tile_quant(grad_full.reshape(total // 128, 128, width), 1).reshape(total, width)
    hidden_grad = jnp.dot(grad_rowq, weight_deq, preferred_element_type=jnp.float32)
    gate_val = gate_pre.astype(jnp.float32)
    up_val = up_pre.astype(jnp.float32)
    sigma = 1.0 / (1.0 + jnp.exp(-gate_val))
    gate_grad = (hidden_grad * up_val * sigma * (1.0 + gate_val * (1.0 - sigma))).astype(jnp.bfloat16)
    up_grad = (hidden_grad * gate_val * sigma).astype(jnp.bfloat16)
    hidden_val = gate_val * sigma * up_val
    hidden_colq = tile_quant(hidden_val.reshape(total // 128, 128, hidden_units), 1).reshape(total, hidden_units)
    grad_reps = grad_colq.reshape(N_DP, TOK, width)
    hidden_reps = hidden_colq.reshape(N_DP, TOK, hidden_units)

    def add_replica(running, pair):
        grad_block, hidden_block = pair
        term = lax.dot_general(grad_block, hidden_block, (((0,), (0,)), ((), ())),
                               preferred_element_type=jnp.float32)
        term = lax.optimization_barrier(term.astype(jnp.bfloat16)).astype(jnp.float32)
        return running + term, None

    summed, _ = lax.scan(add_replica, jnp.zeros((width, hidden_units), jnp.float32), (grad_reps, hidden_reps))
    return gate_grad, up_grad, summed.astype(jnp.bfloat16)
```

```python
import jax
import jax.numpy as jnp
from jax import lax
from jax.experimental import pallas as pl
from jax.experimental.pallas import tpu as pltpu
from jax.sharding import PartitionSpec as P

F32, BF16 = jnp.float32, jnp.bfloat16
D, FFL, TOK = 7168, 384, 128
HALF = D // 2
RING, LINE, REACH = 4, 16, 8
PIECE = HALF // 2
ROWS = 224


def kernel(
    og_ref, gsrc_ref, gate_ref, up_ref, scale_ref, w_hbm,
    gg_ref, ug_ref, dg_ref,
    g1, g1relay, hid, gblk, relay_p, relay_m, g2, g2d, w, acc, dacc,
    hid_recv, hid_send, hid_left, part_send,
    xy_recv, xy_send, blk_recv, near_send, far_send, far_recv, fan_send, anti_sem, w_sem, own_sem,
):
    d = lax.axis_index("dp")
    t = lax.axis_index("tp")
    z, c = d // 2, lax.rem(d, 2)
    h = lax.rem(t, 2)
    q0 = t // 2
    y0, x0 = q0 // RING, lax.rem(q0, RING)
    zf = h * LINE + z
    step_dir = 1 - 2 * c

    def along_z(delta, core):
        pos = lax.rem(zf + delta + 2 * LINE, 2 * LINE)
        return {"dp": lax.rem(pos, LINE) * 2 + core, "tp": q0 * 2 + pos // LINE}

    def in_plane(x, y):
        return {"tp": (y * RING + x) * 2 + h}

    def wrap(v):
        return lax.rem(v + 2 * RING, RING)

    partner = {"dp": d + step_dir}

    def remote(src, dst, ssem, rsem, device):
        return pltpu.make_async_remote_copy(
            src_ref=src, dst_ref=dst, send_sem=ssem, recv_sem=rsem,
            device_id=device, device_id_type=pl.DeviceIdType.MESH,
        )

    barrier = pltpu.get_barrier_semaphore()

    def greet(device):
        pl.semaphore_signal(barrier, inc=1, device_id=device, device_id_type=pl.DeviceIdType.MESH)

    def greet_z(i, carry):
        for core in (0, 1):
            greet(along_z(i, core))
            greet(along_z(-i, core))
        return carry

    lax.fori_loop(1, REACH + 1, greet_z, 0)
    greet(partner)
    for off in (-1, 1):
        greet(in_plane(wrap(x0 + off), y0))
        greet(in_plane(x0, wrap(y0 + off)))
    w_copy = pltpu.make_async_copy(w_hbm, w, w_sem)
    w_copy.start()
    own_copy = pltpu.make_async_copy(og_ref, g1.at[q0, h], own_sem.at[0])
    own_copy.start()
    pl.semaphore_wait(barrier, 4 * REACH + 5)

    def half_rows(half):
        return pl.ds(half * (ROWS // 2), ROWS // 2)

    def unit(k, half, q):
        if k == 2:
            return g2.at[q, half_rows(half)]
        hh = h if k == 0 else 1 - h
        return g1.at[q, hh, :, pl.ds(half * PIECE, PIECE)]

    def own_unit(k, half):
        if k == 0:
            return og_ref.at[:, pl.ds(half * PIECE, PIECE)]
        return unit(k, half, q0)

    def q_of(half, p, s):
        return s * RING + p if half == 0 else p * RING + s

    def dev_of(half, p, s):
        return in_plane(p, s) if half == 0 else in_plane(s, p)

    def xy_send_unit(k, half, idx, q, device, src=None):
        remote(
            unit(k, half, q) if src is None else src, unit(k, half, q),
            xy_send.at[k, half, idx], xy_recv.at[k, half, q], device,
        ).start()

    def xy_wait(k, half, q):
        u = unit(k, half, q)
        remote(u, u, xy_send.at[k, half, 0], xy_recv.at[k, half, q], partner).wait_recv()

    def pos(half):
        return (x0, y0) if half == 0 else (y0, x0)

    def xy_start(k):
        for half in (0, 1):
            p, s = pos(half)
            src = own_unit(k, half)
            pf, pb = wrap(p + step_dir), wrap(p - step_dir)
            sf, sb = wrap(s + step_dir), wrap(s - step_dir)
            xy_send_unit(k, half, 0, q0, dev_of(half, pf, s), src)
            xy_send_unit(k, half, 1, q0, dev_of(half, pb, s), src)
            xy_send_unit(k, half, 2, q0, dev_of(half, p, sf), src)
            xy_send_unit(k, half, 3, q0, dev_of(half, p, sb), src)

    def xy_first(k):
        for stage in (0, 1, 2):
            for half in (0, 1):
                p, s = pos(half)
                pf, pb, po = wrap(p + step_dir), wrap(p - step_dir), wrap(p + 2)
                sf, sb = wrap(s + step_dir), wrap(s - step_dir)
                q = q_of(half, (pb, pf, po)[stage], s)
                xy_wait(k, half, q)
                if stage == 0:
                    xy_send_unit(k, half, 4, q, dev_of(half, pf, s))
                xy_send_unit(k, half, 5 + 2 * stage, q, dev_of(half, p, sf))
                xy_send_unit(k, half, 6 + 2 * stage, q, dev_of(half, p, sb))

    def columns_of(p):
        return (p, wrap(p - step_dir), wrap(p + step_dir), wrap(p + 2))

    def xy_second(k):
        for i in range(RING):
            for half in (0, 1):
                p, s = pos(half)
                sf, sb = wrap(s + step_dir), wrap(s - step_dir)
                q = q_of(half, columns_of(p)[i], sb)
                xy_wait(k, half, q)
                xy_send_unit(k, half, 11 + i, q, dev_of(half, p, sf))

    def xy_last(k):
        for i in range(RING):
            for half in (0, 1):
                p, s = pos(half)
                xy_wait(k, half, q_of(half, columns_of(p)[i], wrap(s + step_dir)))
        for i in range(RING):
            for half in (0, 1):
                p, s = pos(half)
                xy_wait(k, half, q_of(half, columns_of(p)[i], wrap(s + 2)))

    def xy_drain(k):
        for half in (0, 1):
            def one(i, carry, half=half):
                u = unit(k, half, q0)
                remote(u, u, xy_send.at[k, half, i], xy_recv.at[k, half, q0], partner).wait_send()
                return carry

            lax.fori_loop(0, 15, one, 0)

    peer = along_z(step_dir * REACH, c)
    leg1 = remote(og_ref, g1relay, anti_sem.at[0], anti_sem.at[1], peer)
    leg1.start()
    src_pos = lax.rem(zf - step_dir * REACH + 2 * LINE, 2 * LINE)
    leg2 = remote(g1relay, g1.at[q0, src_pos // LINE], anti_sem.at[2], anti_sem.at[3], peer)

    me_slot = (z * 2 + c) * 2 + h

    def far_copy(side):
        first = lax.rem(zf + (REACH + 1 if side == 0 else LINE) + (0 if side == 0 else 0), LINE)
        return remote(
            gsrc_ref.at[pl.ds(first * 2, 2 * REACH)], (relay_p, relay_m)[side],
            far_send.at[side], far_recv.at[side], along_z(REACH if side == 0 else -REACH, c),
        )

    for side in (0, 1):
        far_copy(side).start()
    xy_start(0)

    def near_copy(i, sign, core):
        device = along_z(sign * i, core)
        idx = ((i - 1) * 2 + (0 if sign > 0 else 1)) * 2 + core
        return remote(gsrc_ref.at[device["dp"]], gblk.at[me_slot], near_send.at[idx], blk_recv.at[me_slot], device)

    def near_start(j, carry):
        i = REACH - j
        for sign in (1, -1):
            for core in (0, 1):
                near_copy(i, sign, core).start()
        return carry

    lax.fori_loop(0, REACH, near_start, 0)
    partner_blk = remote(
        gsrc_ref.at[partner["dp"]], gblk.at[me_slot], near_send.at[4 * REACH], blk_recv.at[me_slot], partner
    )
    partner_blk.start()
    own_blk = pltpu.make_async_copy(gsrc_ref.at[d], gblk.at[me_slot], own_sem.at[1])
    own_blk.start()

    gate = gate_ref[...].astype(F32)
    up = up_ref[...].astype(F32)
    hidden = gate * (1.0 / (1.0 + jnp.exp(-gate))) * up
    hscale = (jnp.max(jnp.abs(hidden), axis=0, keepdims=True) + 1e-6) / 448.0
    payload = (hidden / hscale).astype(BF16).astype(F32)
    hid[d] = (payload * hscale).reshape(LINE, 8, FFL).astype(BF16)

    def hid_part(zz, core, sub):
        return hid.at[zz * 2 + core, pl.ds(sub * 8, 8)]

    def hid_copy(zz, core, sub, ssem, device):
        u = hid_part(zz, core, sub)
        return remote(u, u, ssem, hid_recv.at[zz * 2 + core, sub], device)

    right, left = {"dp": lax.rem(d + 2, 2 * LINE)}, {"dp": lax.rem(d + 2 * LINE - 2, 2 * LINE)}
    for sub in (0, 1):
        @pl.when(z < LINE - 1)
        def _():
            hid_copy(z, c, sub, hid_send.at[z, sub], right).start()

        @pl.when(z > 0)
        def _():
            hid_copy(z, c, sub, hid_left.at[sub], left).start()
    for sub in (0, 1):
        hid_copy(z, c, sub, part_send.at[z, sub], partner).start()

    def hid_step(s, carry):
        for sub in (0, 1):
            @pl.when(z - s >= 0)
            def _():
                hid_copy(z - s, c, sub, part_send.at[z - s, sub], partner).wait_recv()

                @pl.when(z < LINE - 1)
                def _():
                    hid_copy(z - s, c, sub, hid_send.at[z - s, sub], right).start()

                hid_copy(z - s, c, sub, part_send.at[z - s, sub], partner).start()

            @pl.when(z + s < LINE)
            def _():
                hid_copy(z + s, c, sub, part_send.at[z + s, sub], partner).wait_recv()

                @pl.when(z > 0)
                def _():
                    hid_copy(z + s, c, sub, hid_send.at[z + s, sub], left).start()

                hid_copy(z + s, c, sub, part_send.at[z + s, sub], partner).start()
        return carry

    def hid_steps(lo, hi):
        lax.fori_loop(lo, hi, hid_step, 0)

    def fan_copy(side, i, core):
        sign = 1 if side == 0 else -1
        src = lax.rem(zf - sign * REACH + 2 * LINE, 2 * LINE)
        slot = (lax.rem(src, LINE) * 2 + c) * 2 + src // LINE
        step = i + 1 if side == 0 else i - REACH
        return remote(
            (relay_p, relay_m)[side].at[i * 2 + core], gblk.at[slot],
            fan_send.at[side, i * 2 + core], blk_recv.at[slot], along_z(step, core),
        )

    def fan_out(side, act):
        last = REACH - 1 if side == 0 else 0

        def one(j, carry):
            i = REACH - 1 - j if side == 0 else j
            for core in (0, 1):
                @pl.when(jnp.logical_or(i != last, c == side))
                def _():
                    act(fan_copy(side, i, core))
            return carry

        lax.fori_loop(0, REACH, one, 0)

    low8 = lax.broadcasted_iota(jnp.int32, (LINE, 8, 128), 1) < 4

    def blocks_to_unit():
        def wait_blk(slot, carry):
            @pl.when(slot != me_slot)
            def _():
                remote(gsrc_ref.at[0], gblk.at[slot], near_send.at[0], blk_recv.at[slot], partner).wait_recv()
            return carry

        lax.fori_loop(0, 4 * LINE, wait_blk, 0)
        own_blk.wait()
        for part in (0, 1):
            v0 = gblk[pl.ds(part * 32, 32)].astype(F32).reshape(16, 2, 8, 128)
            va, vb = v0[:, 0], v0[:, 1]
            first = jnp.where(low8, va, pltpu.roll(vb, 4, 1)).reshape(128, 128)
            second = jnp.where(low8, pltpu.roll(va, 4, 1), vb).reshape(128, 128)
            g2[q0, pl.ds(0, 128), pl.ds(part * 128, 128)] = first.T.astype(BF16)
            g2[q0, pl.ds(128, 96), pl.ds(part * 128, 128)] = second.T[:96].astype(BF16)

    def row_quant(v):
        s = (jnp.max(jnp.abs(v), axis=-1, keepdims=True) + 1e-6) / 448.0
        return ((v * (1.0 / s)).astype(BF16).astype(F32) * s).astype(BF16)

    def grad_tile(l, carry):
        lanes = pl.ds(pl.multiple_of(l * 128, 128), 128)
        va = g1[:, 0, :, lanes].astype(F32)
        vb = g1[:, 1, :, lanes].astype(F32)
        first = jnp.where(low8, va, pltpu.roll(vb, 4, 1)).reshape(TOK, 128)
        second = jnp.where(low8, pltpu.roll(va, 4, 1), vb).reshape(TOK, 128)
        lhs = jnp.concatenate([row_quant(first), row_quant(second)], axis=1)
        rows = pl.ds(pl.multiple_of(l * 128, 128), 128)
        rows2 = pl.ds(pl.multiple_of(HALF + l * 128, 128), 128)
        wa = (w[rows].astype(F32) * scale_ref[pl.ds(l, 1)]).astype(BF16)
        wb = (w[rows2].astype(F32) * scale_ref[pl.ds(l + 28, 1)]).astype(BF16)
        rhs = jnp.concatenate([wa, wb], axis=0)
        acc[...] += jnp.dot(lhs, rhs, preferred_element_type=F32)
        return carry

    def grad_tiles(lo, hi):
        lax.fori_loop(lo, hi, grad_tile, 0)

    def grads_out():
        hg = acc[...]
        g = gate_ref[...].astype(F32)
        u = up_ref[...].astype(F32)
        sg = 1.0 / (1.0 + jnp.exp(-g))
        gg_ref[...] = (hg * u * sg * (1.0 + g * (1.0 - sg))).astype(BF16)
        ug_ref[...] = (hg * g * sg).astype(BF16)

    lane = lax.broadcasted_iota(jnp.int32, (16, 256), 1)

    def col_quant(i, carry):
        rows = pl.ds(pl.multiple_of(i * 16, 16), 16)
        m = jnp.abs(g2[0, rows].astype(F32))
        for q in range(1, LINE):
            m = jnp.maximum(m, jnp.abs(g2[q, rows].astype(F32)))
        for k in (1, 2, 4):
            swapped = jnp.where(lax.rem(lane // k, 2) == 0, pltpu.roll(m, 256 - k, 1), pltpu.roll(m, k, 1))
            m = jnp.maximum(m, swapped)
        s = (m + 1e-6) / 448.0
        inv = 1.0 / s
        for q in range(LINE):
            v = (g2[q, rows].astype(F32) * inv).astype(BF16).astype(F32)
            g2d[q, rows] = (v * s).astype(BF16)
        return carry

    def down_dot(q, carry):
        rhs = hid[:, q].astype(F32).reshape(256, FFL).astype(BF16)
        dacc[...] += jnp.dot(g2d[q], rhs, preferred_element_type=F32)
        return carry

    acc[...] = jnp.zeros_like(acc)
    dacc[...] = jnp.zeros_like(dacc)
    xy_first(0)
    hid_steps(1, 2)
    xy_second(0)
    hid_steps(2, 4)
    for side in (0, 1):
        far_copy(side).wait_recv()
        fan_out(side, lambda copy: copy.start())
    leg1.wait_recv()
    leg2.start()
    hid_steps(4, 7)
    xy_last(0)
    blocks_to_unit()
    xy_start(2)
    hid_steps(7, 8)
    leg2.wait_recv()
    xy_start(1)
    xy_first(2)
    hid_steps(8, 9)
    xy_first(1)
    xy_second(2)
    hid_steps(9, 11)
    xy_second(1)
    xy_last(2)
    hid_steps(11, 12)
    xy_last(1)
    own_copy.wait()
    w_copy.wait()
    grad_tiles(0, 7)
    hid_steps(12, 13)
    grad_tiles(7, 14)
    hid_steps(13, 14)
    grad_tiles(14, 21)
    hid_steps(14, 15)
    grad_tiles(21, 28)
    hid_steps(15, 16)
    lax.fori_loop(0, ROWS // 16, col_quant, 0)
    grads_out()

    def wait_other(zz, carry):
        for sub in (0, 1):
            hid_copy(zz, 1 - c, sub, part_send.at[zz, sub], partner).wait_recv()
        return carry

    lax.fori_loop(0, LINE, wait_other, 0)
    lax.fori_loop(0, LINE, down_dot, 0)
    dg_ref[...] = dacc[...].astype(BF16)

    leg1.wait_send()
    leg2.wait_send()
    for side in (0, 1):
        far_copy(side).wait_send()
        fan_out(side, lambda copy: copy.wait_send())

    def near_drain(i, carry):
        for sign in (1, -1):
            for core in (0, 1):
                near_copy(i, sign, core).wait_send()
        return carry

    lax.fori_loop(1, REACH + 1, near_drain, 0)
    partner_blk.wait_send()
    for k in (0, 1, 2):
        xy_drain(k)

    def hid_drain(zz, carry):
        for sub in (0, 1):
            hid_copy(zz, c, sub, part_send.at[zz, sub], partner).wait_send()

            @pl.when(jnp.logical_or(jnp.logical_and(zz <= z, z < LINE - 1), jnp.logical_and(zz > z, z > 0)))
            def _():
                hid_copy(zz, c, sub, hid_send.at[zz, sub], right).wait_send()
        return carry

    lax.fori_loop(0, LINE, hid_drain, 0)
    for sub in (0, 1):
        @pl.when(z > 0)
        def _():
            hid_copy(z, c, sub, hid_left.at[sub], left).wait_send()


def per_device(out_grad, gate_pre, up_pre, down_weight, block_scales):
    og = out_grad.reshape(4, 2, HALF).transpose(1, 0, 2).reshape(8, HALF)
    blocks = jnp.pad(out_grad.reshape(4, 32, ROWS), ((0, 0), (0, 0), (0, 256 - ROWS)))
    blocks = blocks.reshape(4, 32, 2, 128).transpose(1, 2, 0, 3).reshape(32, 8, 128)
    blocks = jnp.concatenate([blocks, blocks[:16]], axis=0)
    scales = jnp.repeat(block_scales.astype(F32), 128, axis=1)
    vmem = pl.BlockSpec(memory_space=pltpu.VMEM)
    dma = pltpu.SemaphoreType.DMA
    return pl.pallas_call(
        kernel,
        out_shape=(
            jax.ShapeDtypeStruct((TOK, FFL), BF16),
            jax.ShapeDtypeStruct((TOK, FFL), BF16),
            jax.ShapeDtypeStruct((ROWS, FFL), BF16),
        ),
        in_specs=[vmem] * 5 + [pl.BlockSpec(memory_space=pl.ANY)],
        out_specs=(vmem, vmem, vmem),
        scratch_shapes=[
            pltpu.VMEM((16, 2, 8, HALF), BF16),
            pltpu.VMEM((8, HALF), BF16),
            pltpu.VMEM((32, 16, 8, FFL), BF16),
            pltpu.VMEM((64, 8, 128), BF16),
            pltpu.VMEM((16, 8, 128), BF16),
            pltpu.VMEM((16, 8, 128), BF16),
            pltpu.VMEM((16, ROWS, 256), BF16),
            pltpu.VMEM((16, ROWS, 256), BF16),
            pltpu.VMEM((D, FFL), BF16),
            pltpu.VMEM((TOK, FFL), F32),
            pltpu.VMEM((ROWS, FFL), F32),
            dma((32, 2)), dma((16, 2)), dma((2,)), dma((16, 2)),
            dma((3, 2, 16)), dma((3, 2, 15)), dma((64,)), dma((33,)),
            dma((2,)), dma((2,)), dma((2, 16)), dma((4,)), dma, dma((2,)),
        ],
        compiler_params=pltpu.CompilerParams(
            collective_id=0, has_side_effects=True, vmem_limit_bytes=48 * 1024 * 1024
        ),
        name="fused_backward",
    )(og, blocks, gate_pre, up_pre, scales, down_weight)


def solution(mesh):
    placed = (P(("dp", "tp"), None), P("dp", "tp"), P("dp", "tp"), P(None, "tp"), P(None, "tp"))
    return jax.shard_map(
        per_device,
        mesh=mesh,
        in_specs=placed,
        out_specs=(P("dp", "tp"), P("dp", "tp"), P("dp", "tp")),
        check_vma=False,
    )
```

```python
import jax
import jax.numpy as jnp
from jax import lax
from jax.experimental import pallas as pl
from jax.experimental.pallas import tpu as pltpu
from jax.sharding import PartitionSpec as P

F32, BF16 = jnp.float32, jnp.bfloat16
D, FFL, TOK = 7168, 384, 128
HALF = D // 2
RING, LINE, REACH = 4, 16, 8
PIECE = HALF // 2
ROWS = 224


def kernel(
    raw_hbm, gate_hbm, up_hbm, scale_ref, w_hbm,
    gg_ref, ug_ref, dg_ref,
    raw, gate_ref, up_ref, og_ref, gsrc_ref, g1, g1relay, hid, gblk, relay_p, relay_m, g2, g2d, w, acc, dacc,
    hid_recv, hid_send, hid_left, part_send,
    xy_recv, xy_send, blk_recv, near_send, far_send, far_recv, fan_send, anti_sem, w_sem, own_sem, in_sem,
):
    d = lax.axis_index("dp")
    t = lax.axis_index("tp")
    z, c = d // 2, lax.rem(d, 2)
    h = lax.rem(t, 2)
    q0 = t // 2
    y0, x0 = q0 // RING, lax.rem(q0, RING)
    zf = h * LINE + z
    step_dir = 1 - 2 * c

    def along_z(delta, core):
        pos = lax.rem(zf + delta + 2 * LINE, 2 * LINE)
        return {"dp": lax.rem(pos, LINE) * 2 + core, "tp": q0 * 2 + pos // LINE}

    def in_plane(x, y):
        return {"tp": (y * RING + x) * 2 + h}

    def wrap(v):
        return lax.rem(v + 2 * RING, RING)

    partner = {"dp": d + step_dir}

    def remote(src, dst, ssem, rsem, device):
        return pltpu.make_async_remote_copy(
            src_ref=src, dst_ref=dst, send_sem=ssem, recv_sem=rsem,
            device_id=device, device_id_type=pl.DeviceIdType.MESH,
        )

    barrier = pltpu.get_barrier_semaphore()

    def greet(device):
        pl.semaphore_signal(barrier, inc=1, device_id=device, device_id_type=pl.DeviceIdType.MESH)

    def greet_z(i, carry):
        for core in (0, 1):
            greet(along_z(i, core))
            greet(along_z(-i, core))
        return carry

    lax.fori_loop(1, REACH + 1, greet_z, 0)
    greet(partner)
    for off in (-1, 1):
        greet(in_plane(wrap(x0 + off), y0))
        greet(in_plane(x0, wrap(y0 + off)))
    fetches = [
        pltpu.make_async_copy(src, dst, in_sem.at[i])
        for i, (src, dst) in enumerate(((raw_hbm, raw), (gate_hbm, gate_ref), (up_hbm, up_ref)))
    ]
    for fetch in fetches:
        fetch.start()
    w_copy = pltpu.make_async_copy(w_hbm, w, w_sem)
    w_copy.start()

    fetches[0].wait()
    four = raw[...].astype(F32)
    eight = jnp.concatenate([four, four], axis=0)
    low = lax.broadcasted_iota(jnp.int32, (8, 128), 0) < 4
    for i in range(HALF // 128):
        og_ref[:, i * 128:(i + 1) * 128] = jnp.where(
            low, eight[:, i * 128:(i + 1) * 128], eight[:, HALF + i * 128:HALF + (i + 1) * 128]
        ).astype(BF16)
    for i in range(32):
        base, shift = i * ROWS // 128 * 128, i * ROWS % 128
        window = eight[:, base:min(base + 384, D)]
        if shift:
            window = pltpu.roll(window, window.shape[1] - shift, 1)
        block = jnp.where(low, window[:, :128], window[:, 128:256]).astype(BF16)
        gsrc_ref[i] = block
        if i < LINE:
            gsrc_ref[i + 32] = block

    fetches[1].wait()
    fetches[2].wait()
    gate = gate_ref[...].astype(F32)
    up = up_ref[...].astype(F32)
    hidden = gate * (1.0 / (1.0 + jnp.exp(-gate))) * up
    hscale = (jnp.max(jnp.abs(hidden), axis=0, keepdims=True) + 1e-6) / 448.0
    payload = (hidden / hscale).astype(BF16).astype(F32)
    hid[d] = (payload * hscale).reshape(LINE, 8, FFL).astype(BF16)
    acc[...] = jnp.zeros_like(acc)
    dacc[...] = jnp.zeros_like(dacc)
    pl.semaphore_wait(barrier, 4 * REACH + 5)
    own_copy = pltpu.make_async_copy(og_ref, g1.at[q0, h], own_sem.at[0])
    own_copy.start()

    def half_rows(half):
        return pl.ds(half * (ROWS // 2), ROWS // 2)

    def unit(k, half, q):
        if k == 2:
            return g2.at[q, half_rows(half)]
        hh = h if k == 0 else 1 - h
        return g1.at[q, hh, :, pl.ds(half * PIECE, PIECE)]

    def own_unit(k, half):
        if k == 0:
            return og_ref.at[:, pl.ds(half * PIECE, PIECE)]
        return unit(k, half, q0)

    def q_of(half, p, s):
        return s * RING + p if half == 0 else p * RING + s

    def dev_of(half, p, s):
        return in_plane(p, s) if half == 0 else in_plane(s, p)

    def xy_send_unit(k, half, idx, q, device, src=None):
        remote(
            unit(k, half, q) if src is None else src, unit(k, half, q),
            xy_send.at[k, half, idx], xy_recv.at[k, half, q], device,
        ).start()

    def xy_wait(k, half, q):
        u = unit(k, half, q)
        remote(u, u, xy_send.at[k, half, 0], xy_recv.at[k, half, q], partner).wait_recv()

    def pos(half):
        return (x0, y0) if half == 0 else (y0, x0)

    def xy_start(k):
        for half in (0, 1):
            p, s = pos(half)
            src = own_unit(k, half)
            pf, pb = wrap(p + step_dir), wrap(p - step_dir)
            sf, sb = wrap(s + step_dir), wrap(s - step_dir)
            xy_send_unit(k, half, 0, q0, dev_of(half, pf, s), src)
            xy_send_unit(k, half, 1, q0, dev_of(half, pb, s), src)
            xy_send_unit(k, half, 2, q0, dev_of(half, p, sf), src)
            xy_send_unit(k, half, 3, q0, dev_of(half, p, sb), src)

    def columns_of(p):
        return (p, wrap(p - step_dir), wrap(p + step_dir), wrap(p + 2))

    def xy_row(k, half, stage):
        p, s = pos(half)
        q = q_of(half, columns_of(p)[stage], s)
        xy_wait(k, half, q)
        if stage == 1:
            xy_send_unit(k, half, 4, q, dev_of(half, wrap(p + step_dir), s))
        xy_send_unit(k, half, 3 + 2 * stage, q, dev_of(half, p, wrap(s + step_dir)))
        xy_send_unit(k, half, 4 + 2 * stage, q, dev_of(half, p, wrap(s - step_dir)))

    def xy_column(k, half, i):
        p, s = pos(half)
        q = q_of(half, columns_of(p)[i], wrap(s - step_dir))
        xy_wait(k, half, q)
        xy_send_unit(k, half, 11 + i, q, dev_of(half, p, wrap(s + step_dir)))

    def hop1(k):
        for half in (0, 1):
            xy_row(k, half, 1)
            xy_row(k, half, 2)
            xy_column(k, half, 0)

    def hop2(k):
        for half in (0, 1):
            xy_row(k, half, 3)
            xy_column(k, half, 1)
            xy_column(k, half, 2)

    def hop3(k):
        for half in (0, 1):
            xy_column(k, half, 3)

    def xy_last(k):
        for i in range(RING):
            for half in (0, 1):
                p, s = pos(half)
                xy_wait(k, half, q_of(half, columns_of(p)[i], wrap(s + step_dir)))
        for i in range(RING):
            for half in (0, 1):
                p, s = pos(half)
                xy_wait(k, half, q_of(half, columns_of(p)[i], wrap(s + 2)))

    def xy_drain(k):
        for half in (0, 1):
            def one(i, carry, half=half):
                u = unit(k, half, q0)
                remote(u, u, xy_send.at[k, half, i], xy_recv.at[k, half, q0], partner).wait_send()
                return carry

            lax.fori_loop(0, 15, one, 0)

    peer = along_z(step_dir * REACH, c)
    leg1 = remote(og_ref, g1relay, anti_sem.at[0], anti_sem.at[1], peer)
    leg1.start()
    src_pos = lax.rem(zf - step_dir * REACH + 2 * LINE, 2 * LINE)
    leg2 = remote(g1relay, g1.at[q0, src_pos // LINE], anti_sem.at[2], anti_sem.at[3], peer)

    me_slot = (z * 2 + c) * 2 + h

    def far_copy(side):
        first = lax.rem(zf + (REACH + 1 if side == 0 else LINE) + (0 if side == 0 else 0), LINE)
        return remote(
            gsrc_ref.at[pl.ds(first * 2, 2 * REACH)], (relay_p, relay_m)[side],
            far_send.at[side], far_recv.at[side], along_z(REACH if side == 0 else -REACH, c),
        )

    for side in (0, 1):
        far_copy(side).start()
    xy_start(0)

    def near_copy(i, sign, core):
        device = along_z(sign * i, core)
        idx = ((i - 1) * 2 + (0 if sign > 0 else 1)) * 2 + core
        return remote(gsrc_ref.at[device["dp"]], gblk.at[me_slot], near_send.at[idx], blk_recv.at[me_slot], device)

    def near_start(j, carry):
        i = REACH - j
        for sign in (1, -1):
            for core in (0, 1):
                near_copy(i, sign, core).start()
        return carry

    lax.fori_loop(0, REACH, near_start, 0)
    partner_blk = remote(
        gsrc_ref.at[partner["dp"]], gblk.at[me_slot], near_send.at[4 * REACH], blk_recv.at[me_slot], partner
    )
    partner_blk.start()
    own_blk = pltpu.make_async_copy(gsrc_ref.at[d], gblk.at[me_slot], own_sem.at[1])
    own_blk.start()

    def hid_part(zz, core, sub):
        return hid.at[zz * 2 + core, pl.ds(sub * 8, 8)]

    def hid_copy(zz, core, sub, ssem, device):
        u = hid_part(zz, core, sub)
        return remote(u, u, ssem, hid_recv.at[zz * 2 + core, sub], device)

    right, left = {"dp": lax.rem(d + 2, 2 * LINE)}, {"dp": lax.rem(d + 2 * LINE - 2, 2 * LINE)}
    for sub in (0, 1):
        @pl.when(z < LINE - 1)
        def _():
            hid_copy(z, c, sub, hid_send.at[z, sub], right).start()

        @pl.when(z > 0)
        def _():
            hid_copy(z, c, sub, hid_left.at[sub], left).start()
    for sub in (0, 1):
        hid_copy(z, c, sub, part_send.at[z, sub], partner).start()

    def hid_step(s, carry):
        for sub in (0, 1):
            @pl.when(z - s >= 0)
            def _():
                hid_copy(z - s, c, sub, part_send.at[z - s, sub], partner).wait_recv()

                @pl.when(z < LINE - 1)
                def _():
                    hid_copy(z - s, c, sub, hid_send.at[z - s, sub], right).start()

                hid_copy(z - s, c, sub, part_send.at[z - s, sub], partner).start()

            @pl.when(z + s < LINE)
            def _():
                hid_copy(z + s, c, sub, part_send.at[z + s, sub], partner).wait_recv()

                @pl.when(z > 0)
                def _():
                    hid_copy(z + s, c, sub, hid_send.at[z + s, sub], left).start()

                hid_copy(z + s, c, sub, part_send.at[z + s, sub], partner).start()
        return carry

    def hid_steps(lo, hi):
        lax.fori_loop(lo, hi, hid_step, 0)

    def fan_copy(side, i, core):
        sign = 1 if side == 0 else -1
        src = lax.rem(zf - sign * REACH + 2 * LINE, 2 * LINE)
        slot = (lax.rem(src, LINE) * 2 + c) * 2 + src // LINE
        step = i + 1 if side == 0 else i - REACH
        return remote(
            (relay_p, relay_m)[side].at[i * 2 + core], gblk.at[slot],
            fan_send.at[side, i * 2 + core], blk_recv.at[slot], along_z(step, core),
        )

    def fan_out(side, act):
        last = REACH - 1 if side == 0 else 0

        def one(j, carry):
            i = REACH - 1 - j if side == 0 else j
            for core in (0, 1):
                @pl.when(jnp.logical_or(i != last, c == side))
                def _():
                    act(fan_copy(side, i, core))
            return carry

        lax.fori_loop(0, REACH, one, 0)

    low8 = lax.broadcasted_iota(jnp.int32, (LINE, 8, 128), 1) < 4

    def blocks_to_unit():
        def wait_blk(slot, carry):
            @pl.when(slot != me_slot)
            def _():
                remote(gsrc_ref.at[0], gblk.at[slot], near_send.at[0], blk_recv.at[slot], partner).wait_recv()
            return carry

        lax.fori_loop(0, 4 * LINE, wait_blk, 0)
        own_blk.wait()
        for part in (0, 1):
            v0 = gblk[pl.ds(part * 32, 32)].astype(F32).reshape(16, 2, 8, 128)
            va, vb = v0[:, 0], v0[:, 1]
            first = jnp.where(low8, va, pltpu.roll(vb, 4, 1)).reshape(128, 128)
            second = jnp.where(low8, pltpu.roll(va, 4, 1), vb).reshape(128, 128)
            g2[q0, pl.ds(0, 128), pl.ds(part * 128, 128)] = first.T.astype(BF16)
            g2[q0, pl.ds(128, 96), pl.ds(part * 128, 128)] = second.T[:96].astype(BF16)

    def row_quant(v):
        s = (jnp.max(jnp.abs(v), axis=-1, keepdims=True) + 1e-6) / 448.0
        return ((v * (1.0 / s)).astype(BF16).astype(F32) * s).astype(BF16)

    def grad_tile(l, carry):
        lanes = pl.ds(pl.multiple_of(l * 128, 128), 128)
        va = g1[:, 0, :, lanes].astype(F32)
        vb = g1[:, 1, :, lanes].astype(F32)
        first = jnp.where(low8, va, pltpu.roll(vb, 4, 1)).reshape(TOK, 128)
        second = jnp.where(low8, pltpu.roll(va, 4, 1), vb).reshape(TOK, 128)
        lhs = jnp.concatenate([row_quant(first), row_quant(second)], axis=1)
        rows = pl.ds(pl.multiple_of(l * 128, 128), 128)
        rows2 = pl.ds(pl.multiple_of(HALF + l * 128, 128), 128)
        wa = (w[rows].astype(F32) * scale_ref[pl.ds(l, 1)]).astype(BF16)
        wb = (w[rows2].astype(F32) * scale_ref[pl.ds(l + 28, 1)]).astype(BF16)
        rhs = jnp.concatenate([wa, wb], axis=0)
        acc[...] += jnp.dot(lhs, rhs, preferred_element_type=F32)
        return carry

    def grad_tiles(lo, hi):
        lax.fori_loop(lo, hi, grad_tile, 0)

    def grads_out():
        hg = acc[...]
        g = gate_ref[...].astype(F32)
        u = up_ref[...].astype(F32)
        sg = 1.0 / (1.0 + jnp.exp(-g))
        gg_ref[...] = (hg * u * sg * (1.0 + g * (1.0 - sg))).astype(BF16)
        ug_ref[...] = (hg * g * sg).astype(BF16)

    lane = lax.broadcasted_iota(jnp.int32, (16, 256), 1)

    def col_quant(i, carry):
        rows = pl.ds(pl.multiple_of(i * 16, 16), 16)
        m = jnp.abs(g2[0, rows].astype(F32))
        for q in range(1, LINE):
            m = jnp.maximum(m, jnp.abs(g2[q, rows].astype(F32)))
        for k in (1, 2, 4):
            swapped = jnp.where(lax.rem(lane // k, 2) == 0, pltpu.roll(m, 256 - k, 1), pltpu.roll(m, k, 1))
            m = jnp.maximum(m, swapped)
        s = (m + 1e-6) / 448.0
        inv = 1.0 / s
        for q in range(LINE):
            v = (g2[q, rows].astype(F32) * inv).astype(BF16).astype(F32)
            g2d[q, rows] = (v * s).astype(BF16)
        return carry

    def down_dot(q, carry):
        rhs = hid[:, q].astype(F32).reshape(256, FFL).astype(BF16)
        dacc[...] += jnp.dot(g2d[q], rhs, preferred_element_type=F32)
        return carry

    hid_steps(1, 2)
    hop1(0)
    hid_steps(2, 3)
    hop2(0)
    hid_steps(3, 4)
    hop3(0)
    leg1.wait_recv()
    leg2.start()
    for side in (0, 1):
        far_copy(side).wait_recv()
        fan_out(side, lambda copy: copy.start())
    hid_steps(4, 7)
    leg2.wait_recv()
    xy_start(1)
    blocks_to_unit()
    xy_start(2)
    hid_steps(7, 8)
    xy_last(0)
    hop1(1)
    hop1(2)
    hid_steps(8, 9)
    hop2(1)
    hop2(2)
    hid_steps(9, 10)
    hop3(1)
    hop3(2)
    hid_steps(10, 12)
    xy_last(1)
    xy_last(2)
    own_copy.wait()
    w_copy.wait()
    grad_tiles(0, 10)
    hid_steps(12, 13)
    grad_tiles(10, 20)
    hid_steps(13, 14)
    grad_tiles(20, 28)
    grads_out()
    hid_steps(14, 15)
    lax.fori_loop(0, ROWS // 16, col_quant, 0)
    hid_steps(15, 16)

    def wait_other(zz, carry):
        for sub in (0, 1):
            hid_copy(zz, 1 - c, sub, part_send.at[zz, sub], partner).wait_recv()
        return carry

    lax.fori_loop(0, LINE, wait_other, 0)
    lax.fori_loop(0, LINE, down_dot, 0)
    dg_ref[...] = dacc[...].astype(BF16)

    leg1.wait_send()
    leg2.wait_send()
    for side in (0, 1):
        far_copy(side).wait_send()
        fan_out(side, lambda copy: copy.wait_send())

    def near_drain(i, carry):
        for sign in (1, -1):
            for core in (0, 1):
                near_copy(i, sign, core).wait_send()
        return carry

    lax.fori_loop(1, REACH + 1, near_drain, 0)
    partner_blk.wait_send()
    for k in (0, 1, 2):
        xy_drain(k)

    def hid_drain(zz, carry):
        for sub in (0, 1):
            hid_copy(zz, c, sub, part_send.at[zz, sub], partner).wait_send()

            @pl.when(jnp.logical_or(jnp.logical_and(zz <= z, z < LINE - 1), jnp.logical_and(zz > z, z > 0)))
            def _():
                hid_copy(zz, c, sub, hid_send.at[zz, sub], right).wait_send()
        return carry

    lax.fori_loop(0, LINE, hid_drain, 0)
    for sub in (0, 1):
        @pl.when(z > 0)
        def _():
            hid_copy(z, c, sub, hid_left.at[sub], left).wait_send()


def per_device(out_grad, gate_pre, up_pre, down_weight, block_scales):
    scales = jnp.repeat(block_scales.astype(F32), 128, axis=1)
    vmem = pl.BlockSpec(memory_space=pltpu.VMEM)
    hbm = pl.BlockSpec(memory_space=pl.ANY)
    dma = pltpu.SemaphoreType.DMA
    return pl.pallas_call(
        kernel,
        out_shape=(
            jax.ShapeDtypeStruct((TOK, FFL), BF16),
            jax.ShapeDtypeStruct((TOK, FFL), BF16),
            jax.ShapeDtypeStruct((ROWS, FFL), BF16),
        ),
        in_specs=[hbm] * 3 + [vmem, hbm],
        out_specs=(vmem, vmem, vmem),
        scratch_shapes=[
            pltpu.VMEM((4, D), BF16),
            pltpu.VMEM((TOK, FFL), BF16),
            pltpu.VMEM((TOK, FFL), BF16),
            pltpu.VMEM((8, HALF), BF16),
            pltpu.VMEM((48, 8, 128), BF16),
            pltpu.VMEM((16, 2, 8, HALF), BF16),
            pltpu.VMEM((8, HALF), BF16),
            pltpu.VMEM((32, 16, 8, FFL), BF16),
            pltpu.VMEM((64, 8, 128), BF16),
            pltpu.VMEM((16, 8, 128), BF16),
            pltpu.VMEM((16, 8, 128), BF16),
            pltpu.VMEM((16, ROWS, 256), BF16),
            pltpu.VMEM((16, ROWS, 256), BF16),
            pltpu.VMEM((D, FFL), BF16),
            pltpu.VMEM((TOK, FFL), F32),
            pltpu.VMEM((ROWS, FFL), F32),
            dma((32, 2)), dma((16, 2)), dma((2,)), dma((16, 2)),
            dma((3, 2, 16)), dma((3, 2, 15)), dma((64,)), dma((33,)),
            dma((2,)), dma((2,)), dma((2, 16)), dma((4,)), dma, dma((2,)), dma((3,)),
        ],
        compiler_params=pltpu.CompilerParams(
            collective_id=0, has_side_effects=True, vmem_limit_bytes=48 * 1024 * 1024
        ),
        name="fused_backward",
    )(out_grad, gate_pre, up_pre, scales, down_weight)


def solution(mesh):
    placed = (P(("dp", "tp"), None), P("dp", "tp"), P("dp", "tp"), P(None, "tp"), P(None, "tp"))
    return jax.shard_map(
        per_device,
        mesh=mesh,
        in_specs=placed,
        out_specs=(P("dp", "tp"), P("dp", "tp"), P("dp", "tp")),
        check_vma=False,
    )
```

```python
import jax
import jax.numpy as jnp
from jax import lax
from jax.experimental import pallas as pl
from jax.experimental.pallas import tpu as pltpu
from jax.sharding import PartitionSpec as P

F32, BF16 = jnp.float32, jnp.bfloat16
D, FFL, TOK = 7168, 384, 128
HALF = D // 2
RING, LINE, REACH = 4, 16, 8
PIECE = HALF // 2
ROWS = 224


def kernel(
    raw_hbm, gate_hbm, up_hbm, scale_ref, w_hbm,
    gg_ref, ug_ref, dg_ref,
    raw, gate_ref, up_ref, og_ref, gsrc_ref, g1, g1relay, hid, gblk, gpart, relay_p, relay_m, g2, g2d, w, acc, dacc,
    hid_recv, hid_send, hid_left, part_send,
    xy_recv, xy_send, blk_recv, part_recv, near_send, far_send, far_recv, fan_send, anti_sem, w_sem, own_sem, in_sem,
):
    d = lax.axis_index("dp")
    t = lax.axis_index("tp")
    z, c = d // 2, lax.rem(d, 2)
    h = lax.rem(t, 2)
    q0 = t // 2
    y0, x0 = q0 // RING, lax.rem(q0, RING)
    zf = h * LINE + z
    step_dir = 1 - 2 * c

    def along_z(delta, core):
        pos = lax.rem(zf + delta + 2 * LINE, 2 * LINE)
        return {"dp": lax.rem(pos, LINE) * 2 + core, "tp": q0 * 2 + pos // LINE}

    def in_plane(x, y):
        return {"tp": (y * RING + x) * 2 + h}

    def wrap(v):
        return lax.rem(v + 2 * RING, RING)

    partner = {"dp": d + step_dir}

    def remote(src, dst, ssem, rsem, device):
        return pltpu.make_async_remote_copy(
            src_ref=src, dst_ref=dst, send_sem=ssem, recv_sem=rsem,
            device_id=device, device_id_type=pl.DeviceIdType.MESH,
        )

    barrier = pltpu.get_barrier_semaphore()

    def greet(device):
        pl.semaphore_signal(barrier, inc=1, device_id=device, device_id_type=pl.DeviceIdType.MESH)

    def greet_z(i, carry):
        greet(along_z(i, c))
        greet(along_z(-i, c))
        return carry

    lax.fori_loop(1, REACH + 1, greet_z, 0)
    greet(partner)
    for off in (-1, 1):
        greet(in_plane(wrap(x0 + off), y0))
        greet(in_plane(x0, wrap(y0 + off)))
    fetches = [
        pltpu.make_async_copy(src, dst, in_sem.at[i])
        for i, (src, dst) in enumerate(((raw_hbm, raw), (gate_hbm, gate_ref), (up_hbm, up_ref)))
    ]
    for fetch in fetches:
        fetch.start()
    w_copy = pltpu.make_async_copy(w_hbm, w, w_sem)
    w_copy.start()

    fetches[0].wait()
    four = raw[...].astype(F32)
    eight = jnp.concatenate([four, four], axis=0)
    low = lax.broadcasted_iota(jnp.int32, (8, 128), 0) < 4
    for i in range(HALF // 128):
        og_ref[:, i * 128:(i + 1) * 128] = jnp.where(
            low, eight[:, i * 128:(i + 1) * 128], eight[:, HALF + i * 128:HALF + (i + 1) * 128]
        ).astype(BF16)
    for i in range(32):
        base, shift = i * ROWS // 128 * 128, i * ROWS % 128
        window = eight[:, base:min(base + 384, D)]
        if shift:
            window = pltpu.roll(window, window.shape[1] - shift, 1)
        block = jnp.where(low, window[:, :128], window[:, 128:256]).astype(BF16)
        gsrc_ref[i] = block
        if i < LINE:
            gsrc_ref[i + 32] = block

    fetches[1].wait()
    fetches[2].wait()
    gate = gate_ref[...].astype(F32)
    up = up_ref[...].astype(F32)
    hidden = gate * (1.0 / (1.0 + jnp.exp(-gate))) * up
    hscale = (jnp.max(jnp.abs(hidden), axis=0, keepdims=True) + 1e-6) / 448.0
    payload = (hidden / hscale).astype(BF16).astype(F32)
    hid[c * LINE + z] = (payload * hscale).reshape(LINE, 8, FFL).astype(BF16)
    acc[...] = jnp.zeros_like(acc)
    dacc[...] = jnp.zeros_like(dacc)
    pl.semaphore_wait(barrier, 2 * REACH + 5)
    own_copy = pltpu.make_async_copy(og_ref, g1.at[q0, h], own_sem.at[0])
    own_copy.start()

    def half_rows(half):
        return pl.ds(half * (ROWS // 2), ROWS // 2)

    def unit(k, half, q):
        if k == 2:
            return g2.at[q, half_rows(half)]
        hh = h if k == 0 else 1 - h
        return g1.at[q, hh, :, pl.ds(half * PIECE, PIECE)]

    def own_unit(k, half):
        if k == 0:
            return og_ref.at[:, pl.ds(half * PIECE, PIECE)]
        return unit(k, half, q0)

    def q_of(half, p, s):
        return s * RING + p if half == 0 else p * RING + s

    def dev_of(half, p, s):
        return in_plane(p, s) if half == 0 else in_plane(s, p)

    def xy_send_unit(k, half, idx, q, device, src=None):
        remote(
            unit(k, half, q) if src is None else src, unit(k, half, q),
            xy_send.at[k, half, idx], xy_recv.at[k, half, q], device,
        ).start()

    def xy_wait(k, half, q):
        u = unit(k, half, q)
        remote(u, u, xy_send.at[k, half, 0], xy_recv.at[k, half, q], partner).wait_recv()

    def pos(half):
        return (x0, y0) if half == 0 else (y0, x0)

    def xy_start(k):
        for half in (0, 1):
            p, s = pos(half)
            src = own_unit(k, half)
            pf, pb = wrap(p + step_dir), wrap(p - step_dir)
            sf, sb = wrap(s + step_dir), wrap(s - step_dir)
            xy_send_unit(k, half, 0, q0, dev_of(half, pf, s), src)
            xy_send_unit(k, half, 1, q0, dev_of(half, pb, s), src)
            xy_send_unit(k, half, 2, q0, dev_of(half, p, sf), src)
            xy_send_unit(k, half, 3, q0, dev_of(half, p, sb), src)

    def columns_of(p):
        return (p, wrap(p - step_dir), wrap(p + step_dir), wrap(p + 2))

    def xy_row(k, half, stage):
        p, s = pos(half)
        q = q_of(half, columns_of(p)[stage], s)
        xy_wait(k, half, q)
        if stage == 1:
            xy_send_unit(k, half, 4, q, dev_of(half, wrap(p + step_dir), s))
        xy_send_unit(k, half, 3 + 2 * stage, q, dev_of(half, p, wrap(s + step_dir)))
        xy_send_unit(k, half, 4 + 2 * stage, q, dev_of(half, p, wrap(s - step_dir)))

    def xy_column(k, half, i):
        p, s = pos(half)
        q = q_of(half, columns_of(p)[i], wrap(s - step_dir))
        xy_wait(k, half, q)
        xy_send_unit(k, half, 11 + i, q, dev_of(half, p, wrap(s + step_dir)))

    def hop1(k):
        for half in (0, 1):
            xy_row(k, half, 1)
            xy_row(k, half, 2)
            xy_column(k, half, 0)

    def hop2(k):
        for half in (0, 1):
            xy_row(k, half, 3)
            xy_column(k, half, 1)
            xy_column(k, half, 2)

    def hop3(k):
        for half in (0, 1):
            xy_column(k, half, 3)

    def xy_last(k):
        for i in range(RING):
            for half in (0, 1):
                p, s = pos(half)
                xy_wait(k, half, q_of(half, columns_of(p)[i], wrap(s + step_dir)))
        for i in range(RING):
            for half in (0, 1):
                p, s = pos(half)
                xy_wait(k, half, q_of(half, columns_of(p)[i], wrap(s + 2)))

    def xy_drain(k):
        for half in (0, 1):
            def one(i, carry, half=half):
                u = unit(k, half, q0)
                remote(u, u, xy_send.at[k, half, i], xy_recv.at[k, half, q0], partner).wait_send()
                return carry

            lax.fori_loop(0, 15, one, 0)

    def hid_part(zz, core, sub):
        return hid.at[core * LINE + zz, pl.ds(sub * 4, 4)]

    def hid_copy(zz, core, sub, ssem, device):
        u = hid_part(zz, core, sub)
        return remote(u, u, ssem, hid_recv.at[zz * 2 + core, sub], device)

    right, left = {"dp": lax.rem(d + 2, 2 * LINE)}, {"dp": lax.rem(d + 2 * LINE - 2, 2 * LINE)}
    for sub in range(4):
        @pl.when(z < LINE - 1)
        def _():
            hid_copy(z, c, sub, hid_send.at[z, sub], right).start()

        @pl.when(z > 0)
        def _():
            hid_copy(z, c, sub, hid_left.at[sub], left).start()
    for sub in range(4):
        hid_copy(z, c, sub, part_send.at[z, sub], partner).start()

    peer = along_z(step_dir * REACH, c)
    leg1 = remote(og_ref, g1relay, anti_sem.at[0], anti_sem.at[1], peer)
    leg1.start()
    src_pos = lax.rem(zf - step_dir * REACH + 2 * LINE, 2 * LINE)
    leg2 = remote(g1relay, g1.at[q0, src_pos // LINE], anti_sem.at[2], anti_sem.at[3], peer)

    me_slot = z * 2 + h

    def far_copy(side):
        first = lax.rem(zf + (REACH + 1 if side == 0 else LINE) + (0 if side == 0 else 0), LINE)
        return remote(
            gsrc_ref.at[pl.ds(first * 2, 2 * REACH)], (relay_p, relay_m)[side],
            far_send.at[side], far_recv.at[side], along_z(REACH if side == 0 else -REACH, c),
        )

    for side in (0, 1):
        far_copy(side).start()
    xy_start(0)

    def pair_of(zz):
        return gsrc_ref.at[pl.ds(zz * 2, 2)]

    def near_copy(i, sign):
        idx = (i - 1) * 2 + (0 if sign > 0 else 1)
        to = lax.rem(zf + sign * i + 2 * LINE, LINE)
        return remote(pair_of(to), gblk.at[me_slot], near_send.at[idx], blk_recv.at[me_slot], along_z(sign * i, c))

    def near_start(j, carry):
        for sign in (1, -1):
            near_copy(REACH - j, sign).start()
        return carry

    own_blk = pltpu.make_async_copy(pair_of(z), gblk.at[me_slot], own_sem.at[1])
    own_blk.start()

    def hid_step(s, carry):
        for sub in range(4):
            @pl.when(z - s >= 0)
            def _():
                hid_copy(z - s, c, sub, part_send.at[z - s, sub], partner).wait_recv()

                @pl.when(z < LINE - 1)
                def _():
                    hid_copy(z - s, c, sub, hid_send.at[z - s, sub], right).start()

                hid_copy(z - s, c, sub, part_send.at[z - s, sub], partner).start()

            @pl.when(z + s < LINE)
            def _():
                hid_copy(z + s, c, sub, part_send.at[z + s, sub], partner).wait_recv()

                @pl.when(z > 0)
                def _():
                    hid_copy(z + s, c, sub, hid_send.at[z + s, sub], left).start()

                hid_copy(z + s, c, sub, part_send.at[z + s, sub], partner).start()
        return carry

    def hid_steps(lo, hi):
        lax.fori_loop(lo, hi, hid_step, 0)

    def fan_copy(side, i):
        sign = 1 if side == 0 else -1
        src = lax.rem(zf - sign * REACH + 2 * LINE, 2 * LINE)
        slot = lax.rem(src, LINE) * 2 + src // LINE
        step = i + 1 if side == 0 else i - REACH
        return remote(
            (relay_p, relay_m)[side].at[pl.ds(i * 2, 2)], gblk.at[slot],
            fan_send.at[side, i], blk_recv.at[slot], along_z(step, c),
        )

    def fan_out(side, act):
        last = REACH - 1 if side == 0 else 0

        def one(j, carry):
            i = REACH - 1 - j if side == 0 else j

            @pl.when(jnp.logical_or(i != last, c == side))
            def _():
                act(fan_copy(side, i))
            return carry

        lax.fori_loop(0, REACH, one, 0)

    low8 = lax.broadcasted_iota(jnp.int32, (LINE, 8, 128), 1) < 4

    swap = remote(gblk.at[:, 1 - c], gpart, near_send.at[2 * REACH], part_recv, partner)

    def blocks_swap():
        def wait_blk(slot, carry):
            @pl.when(slot != me_slot)
            def _():
                remote(pair_of(0), gblk.at[slot], near_send.at[0], blk_recv.at[slot], partner).wait_recv()
            return carry

        own_blk.wait()
        lax.fori_loop(0, 2 * LINE, wait_blk, 0)
        swap.start()

    def side_to_unit(blocks, core):
        v0 = blocks.astype(F32).reshape(LINE, 2, 8, 128)
        va, vb = v0[:, 0], v0[:, 1]
        first = jnp.where(low8, va, pltpu.roll(vb, 4, 1)).reshape(128, 128)
        second = jnp.where(low8, pltpu.roll(va, 4, 1), vb).reshape(128, 128)
        lanes = pl.ds(pl.multiple_of(core * 128, 128), 128)
        g2[q0, pl.ds(0, 128), lanes] = first.T.astype(BF16)
        g2[q0, pl.ds(128, 96), lanes] = second.T[:96].astype(BF16)

    def blocks_to_unit():
        side_to_unit(gblk[:, c], c)
        swap.wait_recv()
        side_to_unit(gpart[...], 1 - c)

    def row_quant(v):
        s = (jnp.max(jnp.abs(v), axis=-1, keepdims=True) + 1e-6) / 448.0
        return ((v * (1.0 / s)).astype(BF16).astype(F32) * s).astype(BF16)

    def grad_tile(l, carry):
        lanes = pl.ds(pl.multiple_of(l * 128, 128), 128)
        va = g1[:, 0, :, lanes].astype(F32)
        vb = g1[:, 1, :, lanes].astype(F32)
        first = jnp.where(low8, va, pltpu.roll(vb, 4, 1)).reshape(TOK, 128)
        second = jnp.where(low8, pltpu.roll(va, 4, 1), vb).reshape(TOK, 128)
        lhs = jnp.concatenate([row_quant(first), row_quant(second)], axis=1)
        rows = pl.ds(pl.multiple_of(l * 128, 128), 128)
        rows2 = pl.ds(pl.multiple_of(HALF + l * 128, 128), 128)
        wa = (w[rows].astype(F32) * scale_ref[pl.ds(l, 1)]).astype(BF16)
        wb = (w[rows2].astype(F32) * scale_ref[pl.ds(l + 28, 1)]).astype(BF16)
        rhs = jnp.concatenate([wa, wb], axis=0)
        acc[...] += jnp.dot(lhs, rhs, preferred_element_type=F32)
        return carry

    def grad_tiles(lo, hi):
        lax.fori_loop(lo, hi, grad_tile, 0)

    def grads_out():
        hg = acc[...]
        g = gate_ref[...].astype(F32)
        u = up_ref[...].astype(F32)
        sg = 1.0 / (1.0 + jnp.exp(-g))
        gg_ref[...] = (hg * u * sg * (1.0 + g * (1.0 - sg))).astype(BF16)
        ug_ref[...] = (hg * g * sg).astype(BF16)

    lane = lax.broadcasted_iota(jnp.int32, (16, 256), 1)

    def col_quant(i, carry):
        rows = pl.ds(pl.multiple_of(i * 16, 16), 16)
        m = jnp.abs(g2[0, rows].astype(F32))
        for q in range(1, LINE):
            m = jnp.maximum(m, jnp.abs(g2[q, rows].astype(F32)))
        for k in (1, 2, 4):
            swapped = jnp.where(lax.rem(lane // k, 2) == 0, pltpu.roll(m, 256 - k, 1), pltpu.roll(m, k, 1))
            m = jnp.maximum(m, swapped)
        s = (m + 1e-6) / 448.0
        inv = 1.0 / s
        for q in range(LINE):
            v = (g2[q, rows].astype(F32) * inv).astype(BF16).astype(F32)
            g2d[q, rows] = (v * s).astype(BF16)
        return carry

    def down_dot(j, carry):
        total = dacc[...]
        for i in range(4):
            q = j * 4 + i
            rhs = hid[:, q].astype(F32).reshape(256, FFL).astype(BF16)
            total += jnp.dot(g2d[q], rhs, preferred_element_type=F32)
        dacc[...] = total
        return carry

    hid_steps(1, 2)
    lax.fori_loop(0, 3, near_start, 0)
    hop1(0)
    hid_steps(2, 3)
    lax.fori_loop(3, 5, near_start, 0)
    hop2(0)
    hid_steps(3, 4)
    lax.fori_loop(5, 8, near_start, 0)
    hop3(0)
    leg1.wait_recv()
    leg2.start()
    for side in (0, 1):
        far_copy(side).wait_recv()
        fan_out(side, lambda copy: copy.start())
    hid_steps(4, 7)
    blocks_swap()
    leg2.wait_recv()
    xy_start(1)
    blocks_to_unit()
    xy_start(2)
    hid_steps(7, 8)
    xy_last(0)
    hop1(1)
    hop1(2)
    hid_steps(8, 9)
    hop2(1)
    hop2(2)
    hid_steps(9, 10)
    hop3(1)
    hop3(2)
    hid_steps(10, 11)
    own_copy.wait()
    w_copy.wait()
    xy_last(1)
    grad_tiles(0, 7)
    hid_steps(11, 12)
    grad_tiles(7, 14)
    hid_steps(12, 13)
    grad_tiles(14, 21)
    hid_steps(13, 14)
    grad_tiles(21, 28)
    hid_steps(14, 15)
    xy_last(2)
    lax.fori_loop(0, ROWS // 16, col_quant, 0)
    hid_steps(15, 16)
    grads_out()

    def wait_other(zz, carry):
        for sub in range(4):
            hid_copy(zz, 1 - c, sub, part_send.at[zz, sub], partner).wait_recv()
        return carry

    lax.fori_loop(0, LINE, wait_other, 0)
    lax.fori_loop(0, LINE // 4, down_dot, 0)
    dg_ref[...] = dacc[...].astype(BF16)

    leg1.wait_send()
    leg2.wait_send()
    for side in (0, 1):
        far_copy(side).wait_send()
        fan_out(side, lambda copy: copy.wait_send())

    def near_drain(i, carry):
        for sign in (1, -1):
            near_copy(i, sign).wait_send()
        return carry

    lax.fori_loop(1, REACH + 1, near_drain, 0)
    swap.wait_send()
    for k in (0, 1, 2):
        xy_drain(k)

    def hid_drain(zz, carry):
        for sub in range(4):
            hid_copy(zz, c, sub, part_send.at[zz, sub], partner).wait_send()

            @pl.when(jnp.logical_or(jnp.logical_and(zz <= z, z < LINE - 1), jnp.logical_and(zz > z, z > 0)))
            def _():
                hid_copy(zz, c, sub, hid_send.at[zz, sub], right).wait_send()
        return carry

    lax.fori_loop(0, LINE, hid_drain, 0)
    for sub in range(4):
        @pl.when(z > 0)
        def _():
            hid_copy(z, c, sub, hid_left.at[sub], left).wait_send()


def per_device(out_grad, gate_pre, up_pre, down_weight, block_scales):
    scales = jnp.repeat(block_scales.astype(F32), 128, axis=1)
    vmem = pl.BlockSpec(memory_space=pltpu.VMEM)
    hbm = pl.BlockSpec(memory_space=pl.ANY)
    dma = pltpu.SemaphoreType.DMA
    return pl.pallas_call(
        kernel,
        out_shape=(
            jax.ShapeDtypeStruct((TOK, FFL), BF16),
            jax.ShapeDtypeStruct((TOK, FFL), BF16),
            jax.ShapeDtypeStruct((ROWS, FFL), BF16),
        ),
        in_specs=[hbm] * 3 + [vmem, hbm],
        out_specs=(vmem, vmem, vmem),
        scratch_shapes=[
            pltpu.VMEM((4, D), BF16),
            pltpu.VMEM((TOK, FFL), BF16),
            pltpu.VMEM((TOK, FFL), BF16),
            pltpu.VMEM((8, HALF), BF16),
            pltpu.VMEM((48, 8, 128), BF16),
            pltpu.VMEM((16, 2, 8, HALF), BF16),
            pltpu.VMEM((8, HALF), BF16),
            pltpu.VMEM((32, 16, 8, FFL), BF16),
            pltpu.VMEM((32, 2, 8, 128), BF16),
            pltpu.VMEM((32, 8, 128), BF16),
            pltpu.VMEM((16, 8, 128), BF16),
            pltpu.VMEM((16, 8, 128), BF16),
            pltpu.VMEM((16, ROWS, 256), BF16),
            pltpu.VMEM((16, ROWS, 256), BF16),
            pltpu.VMEM((D, FFL), BF16),
            pltpu.VMEM((TOK, FFL), F32),
            pltpu.VMEM((ROWS, FFL), F32),
            dma((32, 4)), dma((16, 4)), dma((4,)), dma((16, 4)),
            dma((3, 2, 16)), dma((3, 2, 15)), dma((32,)), dma, dma((17,)),
            dma((2,)), dma((2,)), dma((2, 8)), dma((4,)), dma, dma((2,)), dma((3,)),
        ],
        compiler_params=pltpu.CompilerParams(
            collective_id=0, has_side_effects=True, vmem_limit_bytes=48 * 1024 * 1024
        ),
        name="fused_backward",
    )(out_grad, gate_pre, up_pre, scales, down_weight)


def solution(mesh):
    placed = (P(("dp", "tp"), None), P("dp", "tp"), P("dp", "tp"), P(None, "tp"), P(None, "tp"))
    return jax.shard_map(
        per_device,
        mesh=mesh,
        in_specs=placed,
        out_specs=(P("dp", "tp"), P("dp", "tp"), P("dp", "tp")),
        check_vma=False,
    )
```
